32 devices in a mesh: row: 4 (over z), col: 8 (over y, x, core).
Axes of the slice: x: 2, y: 2, z: 4, core: 2. Of those that a mesh axis runs over, the one named last changes fastest.
Arguments:
- right_side: float32 [2, 16, 512, 512], P(None, None, 'row', 'col'), may hold values from -12 to 12
- symbol: float32 [1024, 1024, 256], P('col', 'row'), may hold values from -0.25 to 4.75, as said below
Outputs:
- solution_field: float32 [2, 16, 512, 512], P(None, None, 'row', 'col')
- residual: float32 [2, 16, 512, 512], P(None, None, 'row', 'col')
The draws below stay inside these ranges and needn't reach their ends.
Inputs may be any that keep to these rules, and one draw needn't show every extreme that they name: For each frequency pair (u, v) the 16 x 16 matrix with entries symbol[u, v, s * 16 + t] is symmetric and positive definite.
All inputs are finite; a program needn't handle non-finite values.
Results may differ from the reference program's by a relative error of at most 0.0003.
Values sent between devices are 32-bit elements; how exact they have to be, the bound alone decides.
A program may use at most 576 MiB of HBM per device.

```python
import math
import jax
import jax.numpy as jnp

BR = 512
BC = 512
SEG = 16
NRHS = 2
ITERS = 1
PR = 1024
PC = 1024


def draw_right_side(key, part):
    rows = jnp.arange(BR, dtype=jnp.float32)[:, None] / max(BR - 1, 1)
    cols = jnp.arange(BC, dtype=jnp.float32)[None, :] / max(BC - 1, 1)
    scale = 1.0 + rows + cols
    shape = (NRHS, SEG, BR, BC)
    base = jnp.clip(jax.random.normal(key, shape, jnp.float32), -4.0, 4.0)
    return base * scale


def draw_symbol(key, part):
    first, second, third = jax.random.split(key, 3)
    shape = (PR, PC, SEG, SEG)
    raw = jax.random.uniform(first, shape, jnp.float32, -1.0, 1.0)
    paired = 0.5 * (raw + jnp.transpose(raw, (0, 1, 3, 2)))
    unit = jnp.eye(SEG, dtype=jnp.float32)[None, None, :, :]
    lifted = jax.random.uniform(second, (PR, PC, SEG, 1), jnp.float32, 1.0, 4.0)
    block = paired * (1.0 - unit) + unit * (SEG - 1.0 + lifted)
    level = jnp.exp(jax.random.uniform(third, (PR, PC), jnp.float32, math.log(0.5), math.log(4.0)))
    return (block * level[:, :, None, None] / SEG).reshape(PR, PC, SEG * SEG)


def setup_inputs(seed: int = 0) -> dict:
    keys = jax.random.split(jax.random.key(seed), 3)
    right_side = draw_right_side(jax.random.fold_in(keys[2], 71), 0)
    symbol = draw_symbol(jax.random.fold_in(keys[2], 71), 0)
    return {"right_side": right_side, "symbol": symbol}


def operate(vector_in, symbol):
    padded = jnp.pad(vector_in, ((0, 0), (0, PR - BR), (0, PC - BC)))
    spectrum = jnp.fft.fft2(padded)
    real_part = jnp.real(spectrum)
    imag_part = jnp.imag(spectrum)
    blocks = symbol.reshape(PR, PC, SEG, SEG)
    mixed_real = jnp.stack([jnp.sum(jnp.transpose(blocks[:, :, index, :], (2, 0, 1)) * real_part, axis=0) for index in range(SEG)])
    mixed_imag = jnp.stack([jnp.sum(jnp.transpose(blocks[:, :, index, :], (2, 0, 1)) * imag_part, axis=0) for index in range(SEG)])
    restored = jnp.fft.ifft2(mixed_real + 1j * mixed_imag)
    return jnp.real(restored)[:, :BR, :BC]


def reference(right_side, symbol):
    solutions = []
    residuals = []
    for index in range(NRHS):
        solution = jnp.zeros_like(right_side[index])
        residual = right_side[index]
        direction = right_side[index]
        norm_now = jnp.sum(residual * residual)
        for iteration in range(ITERS):
            applied = operate(direction, symbol)
            step_size = norm_now / jnp.sum(direction * applied)
            solution = solution + step_size * direction
            residual = residual - step_size * applied
            fresh = jnp.sum(residual * residual)
            direction = residual + (fresh / norm_now) * direction
            norm_now = fresh
        solutions.append(solution)
        residuals.append(residual)
    return jnp.stack(solutions), jnp.stack(residuals)
```

```python
import math

import jax
import jax.numpy as jnp
from jax import lax
from jax.experimental import pallas as pl
from jax.experimental.pallas import tpu as pltpu
from jax.sharding import PartitionSpec as P

PRECISION = lax.Precision.HIGH
ROW_STEP = 8


def tables(phase, length):
    angle = (phase % length).astype(jnp.float32) * (2.0 * math.pi / length)
    return lax.optimization_barrier((jnp.cos(angle), jnp.sin(angle)))


def steps(count, stride=1):
    return jnp.arange(count, dtype=jnp.int32) * stride


def row_transform(freq_rows, rows_all, freq_block):
    fine = math.gcd(32, freq_block)
    place = jnp.tile(steps(rows_all), 2)
    part_in = jnp.repeat(steps(2), rows_all)
    coarse_cos, coarse_sin = tables(steps(freq_rows // fine, fine)[:, None] * place[None, :], freq_rows)
    quarter = (steps(2)[:, None] - part_in[None, :]) * (freq_rows // 4) + freq_rows
    fine_cos, fine_sin = tables(
        steps(fine)[None, :, None] * place[None, None, :] + quarter[:, None, :], freq_rows
    )
    shape = (freq_rows // freq_block, 1, freq_block // fine, 1, 2 * rows_all)
    coarse_cos, coarse_sin = coarse_cos.reshape(shape), coarse_sin.reshape(shape)
    fine_cos, fine_sin = fine_cos[None, :, None], fine_sin[None, :, None]
    return (coarse_cos * fine_cos - coarse_sin * fine_sin).reshape(2 * freq_rows, 2 * rows_all)


def col_transform(freq_cols, cols_all, freq_block, first):
    fine = math.gcd(16, cols_all)
    freq = first + steps(freq_block)
    coarse_cos, coarse_sin = tables(steps(cols_all // fine, fine)[:, None] * freq[None, :], freq_cols)
    quarter = steps(2, freq_cols // 4)[:, None, None]
    fine_cos, fine_sin = tables(steps(fine)[None, :, None] * freq[None, None, :] + quarter, freq_cols)
    coarse_cos, coarse_sin = coarse_cos[None, :, None], coarse_sin[None, :, None]
    fine_cos, fine_sin = fine_cos[:, None], fine_sin[:, None]
    return (coarse_cos * fine_cos - coarse_sin * fine_sin).reshape(2, cols_all, freq_block)


def mix(symbol, spectrum, rhs_count, seg_count):
    freq_rows, freq_cols, pair_count = symbol.shape
    devices, parts, _, width = spectrum.shape
    held = width // freq_cols
    step = math.gcd(ROW_STEP, freq_rows)

    def body(symbol_ref, in_ref, out_ref, turned):
        def one(u, carry):
            turned[...] = symbol_ref[u].T
            sums = {}
            for t in range(seg_count):
                column = turned[t * seg_count : (t + 1) * seg_count, :]
                for part in range(parts):
                    for k in range(rhs_count):
                        owner, at = divmod(k * seg_count + t, held)
                        line = in_ref[owner, part, pl.ds(u, 1), at * freq_cols : (at + 1) * freq_cols]
                        term = column * line
                        sums[part, k] = sums[part, k] + term if t else term
            for part in range(parts):
                for k in range(rhs_count):
                    for s in range(seg_count):
                        owner, at = divmod(k * seg_count + s, held)
                        out_ref[owner, part, pl.ds(u, 1), at * freq_cols : (at + 1) * freq_cols] = sums[
                            part, k
                        ][s : s + 1, :]
            return carry

        lax.fori_loop(0, step, one, 0)

    block = pl.BlockSpec((devices, parts, step, width), lambda i: (0, 0, i, 0))
    return pl.pallas_call(
        body,
        grid=(freq_rows // step,),
        in_specs=[pl.BlockSpec((step, freq_cols, pair_count), lambda i: (i, 0, 0)), block],
        out_specs=block,
        out_shape=jax.ShapeDtypeStruct(spectrum.shape, jnp.float32),
        scratch_shapes=[pltpu.VMEM((pair_count, freq_cols), jnp.float32)],
        name="mix",
    )(symbol, spectrum)


def local(right_side, symbol):
    row_count = lax.axis_size("row")
    col_count = lax.axis_size("col")
    rhs_count, seg_count, row_block, col_block = right_side.shape
    freq_block, freq_width = symbol.shape[:2]
    rows_all = row_block * row_count
    cols_all = col_block * col_count
    freq_rows = freq_block * col_count
    freq_cols = freq_width * row_count
    fields = rhs_count * seg_count
    held = fields // col_count
    to_rows = row_transform(freq_rows, rows_all, freq_block)
    to_cols = col_transform(freq_cols, cols_all, freq_width, lax.axis_index("row") * freq_width)
    flat = right_side.reshape(fields, row_block, col_block)
    whole_cols = lax.all_to_all(flat, "col", split_axis=0, concat_axis=2, tiled=True)
    whole = lax.all_gather(whole_cols, "row", axis=1, tiled=True)
    half = jnp.einsum("prc,zcv->zrpv", whole, to_cols, precision=PRECISION)
    half = half.reshape(2 * rows_all, held * freq_width)
    spectrum = jnp.dot(to_rows, half, precision=PRECISION)
    spectrum = spectrum.reshape(col_count, 2, freq_block, held * freq_width)
    spectrum = lax.all_to_all(spectrum, "col", split_axis=0, concat_axis=0, tiled=True)
    mixed = mix(symbol, spectrum, rhs_count, seg_count)
    mixed = lax.all_to_all(mixed, "col", split_axis=0, concat_axis=0, tiled=True)
    mixed = mixed.reshape(2 * freq_rows, held * freq_width)
    back = lax.dot_general(to_rows, mixed, (((0,), (0,)), ((), ())), precision=PRECISION)
    back = back.reshape(2, rows_all, held, freq_width)
    image = jnp.einsum("zrpv,zcv->prc", back, to_cols, precision=PRECISION)
    image = lax.psum_scatter(image, "row", scatter_dimension=1, tiled=True)
    applied = lax.all_to_all(image, "col", split_axis=2, concat_axis=0, tiled=True)
    applied = applied.reshape(right_side.shape) * (1.0 / (freq_rows * freq_cols))
    norm_now, curve = lax.psum(
        (
            jnp.sum(right_side * right_side, axis=(1, 2, 3)),
            jnp.sum(right_side * applied, axis=(1, 2, 3)),
        ),
        ("row", "col"),
    )
    step_size = (norm_now / curve)[:, None, None, None]
    return (step_size * right_side, right_side - step_size * applied)


def solution(mesh):
    placed = P(None, None, "row", "col")
    return jax.shard_map(
        local,
        mesh=mesh,
        in_specs=(placed, P("col", "row", None)),
        out_specs=(placed, placed),
        check_vma=False,
    )
```

```python
import math

import jax
import jax.numpy as jnp
from jax import lax
from jax.experimental import pallas as pl
from jax.experimental.pallas import tpu as pltpu
from jax.sharding import PartitionSpec as P

PRECISION = lax.Precision.HIGH
ROW_STEP = 8


def tables(phase, length):
    angle = (phase % length).astype(jnp.float32) * (2.0 * math.pi / length)
    return lax.optimization_barrier((jnp.cos(angle), jnp.sin(angle)))


def steps(count, stride=1):
    return jnp.arange(count, dtype=jnp.int32) * stride


def row_transform(freq_rows, rows_all, freq_block):
    fine = math.gcd(32, freq_block)
    place = jnp.tile(steps(rows_all), 2)
    part_in = jnp.repeat(steps(2), rows_all)
    coarse_cos, coarse_sin = tables(steps(freq_rows // fine, fine)[:, None] * place[None, :], freq_rows)
    quarter = (steps(2)[:, None] - part_in[None, :]) * (freq_rows // 4) + freq_rows
    fine_cos, fine_sin = tables(
        steps(fine)[None, :, None] * place[None, None, :] + quarter[:, None, :], freq_rows
    )
    shape = (freq_rows // freq_block, 1, freq_block // fine, 1, 2 * rows_all)
    coarse_cos, coarse_sin = coarse_cos.reshape(shape), coarse_sin.reshape(shape)
    fine_cos, fine_sin = fine_cos[None, :, None], fine_sin[None, :, None]
    return (coarse_cos * fine_cos - coarse_sin * fine_sin).reshape(2 * freq_rows, 2 * rows_all)


def col_transform(freq_cols, cols_all, freq_block, first):
    fine = math.gcd(16, cols_all)
    freq = first + steps(freq_block)
    coarse_cos, coarse_sin = tables(steps(cols_all // fine, fine)[:, None] * freq[None, :], freq_cols)
    quarter = steps(2, freq_cols // 4)[:, None, None]
    fine_cos, fine_sin = tables(steps(fine)[None, :, None] * freq[None, None, :] + quarter, freq_cols)
    coarse_cos, coarse_sin = coarse_cos[None, :, None], coarse_sin[None, :, None]
    fine_cos, fine_sin = fine_cos[:, None], fine_sin[:, None]
    return (coarse_cos * fine_cos - coarse_sin * fine_sin).reshape(2, cols_all, freq_block)


def mix(symbol, spectra, rhs_count, seg_count):
    freq_rows, freq_cols, pair_count = symbol.shape
    devices, parts, _, width = spectra[0].shape
    count = len(spectra)
    share = width // freq_cols
    step = math.gcd(ROW_STEP, freq_rows)

    def place(field):
        owner, at = divmod(field, share * count)
        group, at = divmod(at, share)
        return group, owner, slice(at * freq_cols, (at + 1) * freq_cols)

    def body(symbol_ref, *refs):
        in_refs, out_refs, turned = refs[:count], refs[count : 2 * count], refs[2 * count]

        def one(u, carry):
            turned[...] = symbol_ref[u].T
            sums = {}
            for t in range(seg_count):
                column = turned[t * seg_count : (t + 1) * seg_count, :]
                for part in range(parts):
                    for k in range(rhs_count):
                        group, owner, lanes = place(k * seg_count + t)
                        term = column * in_refs[group][owner, part, pl.ds(u, 1), lanes]
                        sums[part, k] = sums[part, k] + term if t else term
            for part in range(parts):
                for k in range(rhs_count):
                    for s in range(seg_count):
                        group, owner, lanes = place(k * seg_count + s)
                        out_refs[group][owner, part, pl.ds(u, 1), lanes] = sums[part, k][s : s + 1, :]
            return carry

        lax.fori_loop(0, step, one, 0)

    block = pl.BlockSpec((devices, parts, step, width), lambda i: (0, 0, i, 0))
    return pl.pallas_call(
        body,
        grid=(freq_rows // step,),
        in_specs=[pl.BlockSpec((step, freq_cols, pair_count), lambda i: (i, 0, 0))] + [block] * count,
        out_specs=[block] * count,
        out_shape=[jax.ShapeDtypeStruct(spectra[0].shape, jnp.float32)] * count,
        scratch_shapes=[pltpu.VMEM((pair_count, freq_cols), jnp.float32)],
        name="mix",
    )(symbol, *spectra)


def local(right_side, symbol):
    row_count = lax.axis_size("row")
    col_count = lax.axis_size("col")
    rhs_count, seg_count, row_block, col_block = right_side.shape
    freq_block, freq_width = symbol.shape[:2]
    rows_all = row_block * row_count
    cols_all = col_block * col_count
    freq_rows = freq_block * col_count
    freq_cols = freq_width * row_count
    fields = rhs_count * seg_count
    held = fields // col_count
    to_rows = row_transform(freq_rows, rows_all, freq_block)
    to_cols = col_transform(freq_cols, cols_all, freq_width, lax.axis_index("row") * freq_width)
    count = math.gcd(2, held)
    share = held // count
    norm_factor = 1.0 / (freq_rows * freq_cols)
    flat = right_side.reshape(fields, row_block, col_block)
    whole_cols = lax.all_to_all(flat, "col", split_axis=0, concat_axis=2, tiled=True)
    spectra = []
    for group in range(count):
        own = whole_cols[group * share : (group + 1) * share]
        whole = lax.all_gather(own, "row", axis=1, tiled=True)
        half = jnp.einsum("prc,zcv->zrpv", whole, to_cols, precision=PRECISION)
        half = half.reshape(2 * rows_all, share * freq_width)
        spectrum = jnp.dot(to_rows, half, precision=PRECISION)
        spectrum = spectrum.reshape(col_count, 2, freq_block, share * freq_width)
        spectra.append(lax.all_to_all(spectrum, "col", split_axis=0, concat_axis=0, tiled=True))
    mixtures = mix(symbol, spectra, rhs_count, seg_count)
    sums = []
    for spectrum, mixed in zip(spectra, mixtures):
        for at in range(share):
            lanes = slice(at * freq_width, (at + 1) * freq_width)
            sums.append(jnp.sum(spectrum[..., lanes] * mixed[..., lanes], axis=(1, 2, 3)))
    curve = jnp.stack(sums, axis=1).reshape(rhs_count, seg_count).sum(axis=1) * norm_factor
    norm_now = jnp.sum(right_side * right_side, axis=(1, 2, 3))
    norm_now, curve = lax.psum((norm_now, curve), ("row", "col"))
    images = []
    for mixed in mixtures:
        mixed = lax.all_to_all(mixed, "col", split_axis=0, concat_axis=0, tiled=True)
        mixed, norm_now, curve = lax.optimization_barrier((mixed, norm_now, curve))
        mixed = mixed.reshape(2 * freq_rows, share * freq_width)
        back = lax.dot_general(to_rows, mixed, (((0,), (0,)), ((), ())), precision=PRECISION)
        back = back.reshape(2, rows_all, share, freq_width)
        image = jnp.einsum("zrpv,zcv->prc", back, to_cols, precision=PRECISION)
        images.append(lax.psum_scatter(image, "row", scatter_dimension=1, tiled=True))
    image = jnp.concatenate(images, axis=0)
    applied = lax.all_to_all(image, "col", split_axis=2, concat_axis=0, tiled=True)
    applied = applied.reshape(right_side.shape) * norm_factor
    step_size = (norm_now / curve)[:, None, None, None]
    return (step_size * right_side, right_side - step_size * applied)


def solution(mesh):
    placed = P(None, None, "row", "col")
    return jax.shard_map(
        local,
        mesh=mesh,
        in_specs=(placed, P("col", "row", None)),
        out_specs=(placed, placed),
        check_vma=False,
    )
```
